128 devices in a mesh: il: 8 (over x, core), xl: 16 (over z, y).
Axes of the slice: x: 4, y: 4, z: 4, core: 2. Of those that a mesh axis runs over, the one named last changes fastest.
Arguments:
- traces: bfloat16 [983040, 128], P(('il', 'xl')), may hold values from -6 to 6
- filter_taps: float32 [12, 64], replicated, may hold values from -1.5 to 1.5
- slot_block: int32 [128, 128, 2], P(('il', 'xl')), may hold values from 0 to 59
- slot_cells: int32 [128, 128, 2, 128], P(('il', 'xl')), may hold values from -1 to 1535
- pair_count: int32 [128, 128], P(('il', 'xl')), may hold values from 0 to 2, as said below
Outputs:
- structure_tensor: float32 [6, 256, 768, 128], P(None, 'il', 'xl')
- adjoint_traces: float32 [983040, 128], P(('il', 'xl'))
The draws below stay inside these ranges and needn't reach their ends.
Inputs may be any that keep to these rules, and one draw needn't show every extreme that they name: Slots 0 to pair_count[e, d] - 1 of device e toward tile d are live; at most 2, and for some tiles every device sends 2 live slots.
All inputs are finite; a program needn't handle non-finite values.
Results may differ from the reference program's by a relative error of at most 0.0004.
The reference program's roundings to bfloat16 on the way count: a program that leaves them out, or rounds other values in their place, can miss the bound.
Values may be sent and summed in bfloat16 or wider, within the bound.
A program may use at most 128 MiB of HBM per device.

```python
import jax
import jax.numpy as jnp
from jax import lax

NT = 128
TAPS = 64
NSURV = 12
ROWBLK = 128
BLK_SURV = 5
CIL = 32
CXL = 48
NDEV = 128
NBLK = 60
CAP = 2
CELLS = 1536
NIL = 256
NXL = 768
TRACES = 983040
N_IL = 8
N_XL = 16


def draw_slot_cells(key, part):
    first_key, second_key = jax.random.split(jax.random.fold_in(key, 11))
    cell_ids = jax.random.randint(first_key, (NDEV, NDEV, CAP, ROWBLK), 0, CELLS)
    dropped = jax.random.randint(second_key, (NDEV, NDEV, CAP, ROWBLK), 0, 4) == 0
    return jnp.where(dropped, -1, cell_ids).astype(jnp.int32)


def draw_pair_count(key, part):
    first_key, second_key = jax.random.split(jax.random.fold_in(key, 23))
    ranking = jax.random.permutation(first_key, NDEV)
    heavy = ranking < max(NDEV // 8, 1)
    light = jax.random.randint(second_key, (NDEV, NDEV), 0, CAP)
    return jnp.where(heavy[None, :], CAP, light).astype(jnp.int32)


def with_ends(values, stream_key, least, largest):
    index_at = [jax.random.randint(jax.random.fold_in(stream_key, axis), (), 0, length) for axis, length in enumerate(values.shape)]
    longest = values.shape.index(max(values.shape))
    neighbour = index_at[:longest] + [(index_at[longest] + 1) % values.shape[longest]] + index_at[longest + 1:]
    return values.at[tuple(index_at)].set(least).at[tuple(neighbour)].set(largest)


def level_of(own_key, shape, cuts, low, high):
    level = 1.0
    for position, parts in cuts:
        heights = jax.random.uniform(jax.random.fold_in(jax.random.fold_in(own_key, 6), position), (parts,), jnp.float32, low / len(cuts), high / len(cuts))
        level = level * jnp.repeat(jnp.exp(heights), shape[position] // parts).reshape((-1,) + (1,) * (len(shape) - 1 - position))
    return level


def noise(key, extent, spread, bound, cuts=(), kind=jnp.bfloat16):
    result = spread * jax.random.normal(key, extent, jnp.float32)
    if cuts:
        result = result * level_of(key, extent, cuts, -0.22, 0.18)
    return jnp.clip(result, -bound, bound).astype(kind)


def setup_inputs(seed: int = 0) -> dict:
    splits = jax.random.split(jax.random.key(seed), 6)
    traces = noise(splits[0], (TRACES, NT), 1.0, 6.0, ((0, 128),))
    filter_taps = noise(splits[1], (NSURV, TAPS), 0.25, 1.5, (), jnp.float32)
    slot_block = with_ends(jax.random.randint(splits[2], (NDEV, NDEV, CAP), 0, NBLK), jax.random.fold_in(splits[2], 1), 0, NBLK - 1).astype(jnp.int32)
    slot_cells = draw_slot_cells(jax.random.fold_in(splits[5], 71), 0)
    pair_count = draw_pair_count(jax.random.fold_in(splits[5], 71), 0)
    return {"traces": traces, "filter_taps": filter_taps, "slot_block": slot_block, "slot_cells": slot_cells, "pair_count": pair_count}


def filter_matrices(filter_taps, samples):
    lag_table = jnp.arange(samples, dtype=jnp.int32)[None, :] - jnp.arange(samples, dtype=jnp.int32)[:, None]
    tap_count = filter_taps.shape[1]
    inside = (lag_table >= 0) & (lag_table < tap_count)
    picked = filter_taps[:, jnp.clip(lag_table, 0, tap_count - 1)]
    return jnp.where(inside[None], picked, 0.0).astype(jnp.bfloat16)


def smooth_box(values):
    padded = jnp.pad(values, ((1, 1), (1, 1), (0, 0)))
    box_total = jnp.zeros_like(values)
    for row_shift in range(3):
        for col_shift in range(3):
            box_total = box_total + padded[row_shift:row_shift + values.shape[0], col_shift:col_shift + values.shape[1]]
    return box_total / 9.0


def reference(traces, filter_taps, slot_block, slot_cells, pair_count):
    matrices = filter_matrices(filter_taps, NT)
    by_survey = traces.reshape(NDEV, NSURV, BLK_SURV * ROWBLK, NT)

    def filter_survey(survey):
        inputs = by_survey[:, survey].reshape(NDEV * BLK_SURV * ROWBLK, NT)
        return jnp.dot(inputs, matrices[survey], preferred_element_type=jnp.float32).astype(jnp.bfloat16)

    filtered = lax.map(filter_survey, jnp.arange(NSURV, dtype=jnp.int32))
    filtered = filtered.reshape(NSURV, NDEV, BLK_SURV, ROWBLK, NT).transpose(1, 0, 2, 3, 4).reshape(NDEV, NBLK, ROWBLK, NT)
    slot_live = jnp.arange(CAP, dtype=jnp.int32)[None, None, :] < pair_count[:, :, None]
    live_cells = jnp.where(slot_live[..., None], slot_cells, -1)
    sources = jnp.arange(NDEV, dtype=jnp.int32)

    def stack_tile(target):
        blocks = filtered[sources[:, None], slot_block[:, target, :]]
        cell_ids = live_cells[:, target]
        segment = jnp.where(cell_ids >= 0, cell_ids, CELLS).reshape(-1)
        values = blocks.reshape(-1, NT).astype(jnp.float32)
        stacked = jax.ops.segment_sum(values, segment, CELLS + 1)[:CELLS]
        fold_counts = jax.ops.segment_sum(jnp.ones(segment.shape, jnp.float32), segment, CELLS + 1)[:CELLS]
        return stacked / jnp.maximum(fold_counts, 1.0)[:, None]

    stack_image = lax.map(stack_tile, sources)
    image_half = stack_image.astype(jnp.bfloat16)

    def adjoint_source(source):
        blocks = filtered[source][slot_block[source]]
        cell_ids = live_cells[source]
        is_valid = cell_ids >= 0
        returned = image_half[sources[:, None, None], jnp.where(is_valid, cell_ids, 0)]
        difference = jnp.where(is_valid[..., None], blocks.astype(jnp.float32) - returned.astype(jnp.float32), 0.0)
        residual = jax.ops.segment_sum(difference.reshape(NDEV * CAP, ROWBLK, NT), slot_block[source].reshape(-1), NBLK)
        residual_half = residual.astype(jnp.bfloat16).reshape(NSURV, BLK_SURV * ROWBLK, NT)
        adjoint = jnp.einsum("srt,sut->sru", residual_half.astype(jnp.float32), matrices.astype(jnp.float32), precision=lax.Precision.HIGHEST)
        return adjoint.reshape(NBLK * ROWBLK, NT)

    adjoint_traces = lax.map(adjoint_source, sources).reshape(TRACES, NT)
    grid_image = stack_image.reshape(N_IL, N_XL, CIL, CXL, NT).transpose(0, 2, 1, 3, 4).reshape(NIL, NXL, NT)
    padded = jnp.pad(grid_image, 1)
    grad_il = (padded[2:, 1:-1, 1:-1] - padded[:-2, 1:-1, 1:-1]) * 0.5
    grad_xl = (padded[1:-1, 2:, 1:-1] - padded[1:-1, :-2, 1:-1]) * 0.5
    grad_time = (padded[1:-1, 1:-1, 2:] - padded[1:-1, 1:-1, :-2]) * 0.5
    factor_pairs = ((grad_il, grad_il), (grad_xl, grad_xl), (grad_time, grad_time), (grad_il, grad_xl), (grad_il, grad_time), (grad_xl, grad_time))
    structure_tensor = jnp.stack([smooth_box(left_part * right_part) for left_part, right_part in factor_pairs])
    return (structure_tensor, adjoint_traces)
```

```python
import functools

import jax
import jax.numpy as jnp
from jax import lax
from jax.experimental import pallas as pl
from jax.experimental.pallas import tpu as pltpu
from jax.sharding import PartitionSpec as P

CIL = 32
CXL = 48
LOW = 256
GROUP = 8
BF = jnp.bfloat16
F32 = jnp.float32


def prep_kernel(blocks, traces, rev, out0, out1, filt, mats):
    surveys = mats.shape[0]
    samples = mats.shape[1]
    rows = traces.shape[0] // surveys
    per = rows // samples
    tiles = out0.shape[0]
    step = pl.program_id(0)

    @pl.when(step == 0)
    def _():
        t_id = lax.broadcasted_iota(jnp.int32, (samples, samples), 0)
        u_id = lax.broadcasted_iota(jnp.int32, (samples, samples), 1)
        for s in range(surveys):
            base = jnp.broadcast_to(rev[s : s + 1, :], (samples, samples))
            skew = pltpu.roll(base, 0, 1, stride=1, stride_axis=0)
            mat = jnp.where(u_id <= t_id, skew, 0.0).astype(BF)
            mats[s] = mat
            res = lax.dot_general(
                mat,
                traces[s * rows : (s + 1) * rows, :],
                (((1,), (1,)), ((), ())),
                preferred_element_type=F32,
            ).astype(BF)
            for b in range(per):
                filt[s * per + b] = res[:, b * samples : (b + 1) * samples]

    for k in range(tiles):
        d = step * tiles + k
        out0[k] = filt[blocks[2 * d]]
        out1[k] = filt[blocks[2 * d + 1]]


def prep(traces, rev, blocks, surveys, samples, devices):
    tiles = 8
    nblk = traces.shape[0] // samples
    full = lambda *shape: pl.BlockSpec(shape, lambda i, *_: (0,) * len(shape))
    out = pl.BlockSpec((tiles, samples, samples), lambda i, *_: (i, 0, 0))
    return pl.pallas_call(
        prep_kernel,
        grid_spec=pltpu.PrefetchScalarGridSpec(
            num_scalar_prefetch=1,
            grid=(devices // tiles,),
            in_specs=[full(*traces.shape), full(*rev.shape)],
            out_specs=[
                out,
                out,
                full(nblk, samples, samples),
                full(surveys, samples, samples),
            ],
        ),
        out_shape=[
            jax.ShapeDtypeStruct((devices, samples, samples), BF),
            jax.ShapeDtypeStruct((devices, samples, samples), BF),
            jax.ShapeDtypeStruct((nblk, samples, samples), BF),
            jax.ShapeDtypeStruct((surveys, samples, samples), BF),
        ],
        name="prep",
    )(blocks, traces, rev)


def low_hot(cells, lanes):
    ids = lax.broadcasted_iota(jnp.int32, (LOW, lanes), 0)
    return (ids == (cells & (LOW - 1))).astype(F32).astype(BF)


def fill(cells, data, left, hot):
    group, samples, lanes = data.shape
    highs = (left.shape[0] - 16) // samples
    ids = lax.broadcasted_iota(jnp.int32, (16, lanes), 0)
    for g in range(group):
        at = slice(g * lanes, (g + 1) * lanes)
        here = cells[g : g + 1, :]
        high = here >> 8
        hot[:, at] = low_hot(here, lanes)
        block = data[g]
        masks = (ids == high).astype(F32).astype(BF)
        left[highs * samples :, at] = masks
        for h in range(highs):
            left[h * samples : (h + 1) * samples, at] = block * jnp.broadcast_to(
                (high == h).astype(F32).astype(BF), block.shape
            )


def bin_first_kernel(cells, data, acc, left, hot):
    @pl.when(pl.program_id(0) == 0)
    def _():
        acc[...] = jnp.zeros_like(acc)

    fill(cells, data, left, hot)
    acc[...] += lax.dot_general(
        left[...], hot[...], (((1,), (1,)), ((), ())), preferred_element_type=F32
    )


def bin_last_kernel(cells, data, before, half, image, acc, left, hot):
    @pl.when(pl.program_id(0) == 0)
    def _():
        acc[...] = before[...]

    fill(cells, data, left, hot)
    acc[...] += lax.dot_general(
        left[...], hot[...], (((1,), (1,)), ((), ())), preferred_element_type=F32
    )

    @pl.when(pl.program_id(0) == pl.num_programs(0) - 1)
    def _():
        samples = data.shape[1]
        highs = half.shape[0] // samples
        for h in range(highs):
            fold = acc[highs * samples + h : highs * samples + h + 1, :]
            value = acc[h * samples : (h + 1) * samples, :] / jnp.maximum(fold, 1.0)
            half[h * samples : (h + 1) * samples, :] = value.astype(BF)
            image[h * LOW : (h + 1) * LOW, :] = value.T


def bin_specs(data):
    slots, samples, lanes = data.shape
    cells_spec = pl.BlockSpec((GROUP, lanes), lambda i: (i, 0))
    data_spec = pl.BlockSpec((GROUP, samples, lanes), lambda i: (i, 0, 0))
    return cells_spec, data_spec, slots // GROUP


def bin_first(cells, data, cell_count):
    cells_spec, data_spec, steps = bin_specs(data)
    samples, lanes = data.shape[1:]
    tall = cell_count // LOW * samples + 16
    return pl.pallas_call(
        bin_first_kernel,
        grid=(steps,),
        in_specs=[cells_spec, data_spec],
        out_specs=pl.BlockSpec((tall, LOW), lambda i: (0, 0)),
        out_shape=jax.ShapeDtypeStruct((tall, LOW), F32),
        scratch_shapes=[
            pltpu.VMEM((tall, GROUP * lanes), BF),
            pltpu.VMEM((LOW, GROUP * lanes), BF),
        ],
        cost_estimate=pl.CostEstimate(
            flops=2 * data.shape[0] * lanes * tall * LOW,
            bytes_accessed=data.size * 2,
            transcendentals=0,
        ),
        name="bin_first",
    )(cells, data)


def bin_last(cells, data, before, cell_count):
    cells_spec, data_spec, steps = bin_specs(data)
    samples, lanes = data.shape[1:]
    tall = cell_count // LOW * samples + 16
    return pl.pallas_call(
        bin_last_kernel,
        grid=(steps,),
        in_specs=[cells_spec, data_spec, pl.BlockSpec((tall, LOW), lambda i: (0, 0))],
        out_specs=[
            pl.BlockSpec((tall - 16, LOW), lambda i: (0, 0)),
            pl.BlockSpec((cell_count, samples), lambda i: (0, 0)),
        ],
        out_shape=[
            jax.ShapeDtypeStruct((tall - 16, LOW), BF),
            jax.ShapeDtypeStruct((cell_count, samples), F32),
        ],
        scratch_shapes=[
            pltpu.VMEM((tall, LOW), F32),
            pltpu.VMEM((tall, GROUP * lanes), BF),
            pltpu.VMEM((LOW, GROUP * lanes), BF),
        ],
        cost_estimate=pl.CostEstimate(
            flops=2 * data.shape[0] * lanes * tall * LOW,
            bytes_accessed=data.size * 2,
            transcendentals=0,
        ),
        name="bin_last",
    )(cells, data, before)


def read_kernel(cells, half, out, hot):
    group, samples, lanes = out.shape
    highs = half.shape[0] // samples
    for g in range(group):
        hot[:, g * lanes : (g + 1) * lanes] = low_hot(cells[g : g + 1, :], lanes)
    for g in range(group):
        wide = jnp.dot(
            half[...], hot[:, g * lanes : (g + 1) * lanes], preferred_element_type=F32
        )
        high = jnp.broadcast_to(cells[g : g + 1, :] >> 8, (samples, lanes))
        picked = jnp.zeros((samples, lanes), F32)
        for h in range(highs):
            picked = jnp.where(high == h, wide[h * samples : (h + 1) * samples, :], picked)
        out[g] = picked.astype(BF)


def read(cells, half, samples):
    slots, lanes = cells.shape
    return pl.pallas_call(
        read_kernel,
        grid=(slots // GROUP,),
        in_specs=[
            pl.BlockSpec((GROUP, lanes), lambda i: (i, 0)),
            pl.BlockSpec(half.shape, lambda i: (0, 0)),
        ],
        out_specs=pl.BlockSpec((GROUP, samples, lanes), lambda i: (i, 0, 0)),
        out_shape=jax.ShapeDtypeStruct((slots, samples, lanes), BF),
        scratch_shapes=[pltpu.VMEM((LOW, GROUP * lanes), BF)],
        cost_estimate=pl.CostEstimate(
            flops=2 * slots * lanes * half.size,
            bytes_accessed=slots * lanes * samples * 2,
            transcendentals=0,
        ),
        name="read",
    )(cells, half)


def adjoint_kernel(blocks, block_rows, cells, back0, back1, filt, mats, out, acc):
    nblk, samples, lanes = filt.shape
    tiles = back0.shape[0]
    per = nblk // mats.shape[0]
    step = pl.program_id(0)

    @pl.when(step == 0)
    def _():
        slots = cells.shape[0]
        live = (cells[...] >= 0).astype(F32).astype(BF)
        ids = lax.broadcasted_iota(jnp.int32, (64, slots), 0)
        pick = (ids == block_rows[...]).astype(F32).astype(BF)
        count = jnp.dot(pick, live, preferred_element_type=F32)
        for b in range(nblk):
            acc[b] = filt[b].astype(F32) * count[b : b + 1, :]

    for k in range(tiles):
        d = step * tiles + k
        b0 = blocks[2 * d]
        acc[b0] = acc[b0] - back0[k].astype(F32)
        b1 = blocks[2 * d + 1]
        acc[b1] = acc[b1] - back1[k].astype(F32)

    @pl.when(step == pl.num_programs(0) - 1)
    def _():
        for b in range(nblk):
            out[b * lanes : (b + 1) * lanes, :] = lax.dot_general(
                acc[b].astype(BF),
                mats[b // per],
                (((0,), (0,)), ((), ())),
                preferred_element_type=F32,
            )


def adjoint(blocks, cells, back0, back1, filt, mats):
    tiles = 8
    devices, samples, lanes = back0.shape
    nblk = filt.shape[0]
    full = lambda *shape: pl.BlockSpec(shape, lambda i, *_: (0,) * len(shape))
    back = pl.BlockSpec((tiles, samples, lanes), lambda i, *_: (i, 0, 0))
    return pl.pallas_call(
        adjoint_kernel,
        grid_spec=pltpu.PrefetchScalarGridSpec(
            num_scalar_prefetch=1,
            grid=(devices // tiles,),
            in_specs=[
                full(1, blocks.shape[0]),
                full(*cells.shape),
                back,
                back,
                full(*filt.shape),
                full(*mats.shape),
            ],
            out_specs=full(nblk * lanes, samples),
            scratch_shapes=[pltpu.VMEM((nblk, samples, lanes), F32)],
        ),
        out_shape=jax.ShapeDtypeStruct((nblk * lanes, samples), F32),
        name="adjoint",
    )(blocks, blocks[None, :], cells, back0, back1, filt, mats)


def with_halo(block, sides, width):
    for axis, dim in sides:
        count = lax.axis_size(axis)
        forward = [(i, i + 1) for i in range(count - 1)]
        backward = [(target, source) for source, target in forward]
        low = lax.ppermute(
            lax.slice_in_dim(block, block.shape[dim] - width, None, axis=dim), axis, forward
        )
        high = lax.ppermute(lax.slice_in_dim(block, 0, width, axis=dim), axis, backward)
        block = jnp.concatenate([low, block, high], axis=dim)
    return block


def cycle_box(values, rows_out, cols_out):
    box_total = jnp.zeros((rows_out, cols_out, values.shape[2]), F32)
    for row_shift in range(3):
        for col_shift in range(3):
            box_total = (
                box_total
                + values[row_shift : row_shift + rows_out, col_shift : col_shift + cols_out]
            )
    return box_total / 9.0


def tensor(tile_image):
    count_il = lax.axis_size("il")
    count_xl = lax.axis_size("xl")
    padded = with_halo(tile_image, (("il", 0), ("xl", 1)), 2)
    padded_time = jnp.pad(padded, ((0, 0), (0, 0), (1, 1)))
    grad_il = (padded[2:, 1:-1] - padded[:-2, 1:-1]) * 0.5
    grad_xl = (padded[1:-1, 2:] - padded[1:-1, :-2]) * 0.5
    grad_time = (padded_time[1:-1, 1:-1, 2:] - padded_time[1:-1, 1:-1, :-2]) * 0.5
    rows_il = lax.axis_index("il") * CIL + jnp.arange(CIL + 2, dtype=jnp.int32) - 1
    rows_xl = lax.axis_index("xl") * CXL + jnp.arange(CXL + 2, dtype=jnp.int32) - 1
    inside_il = ((rows_il >= 0) & (rows_il < CIL * count_il)).astype(F32)
    inside_xl = ((rows_xl >= 0) & (rows_xl < CXL * count_xl)).astype(F32)
    cycle_mask = inside_il[:, None, None] * inside_xl[None, :, None]
    factor_pairs = (
        (grad_il, grad_il),
        (grad_xl, grad_xl),
        (grad_time, grad_time),
        (grad_il, grad_xl),
        (grad_il, grad_time),
        (grad_xl, grad_time),
    )
    return jnp.stack(
        [
            cycle_box(left_part * right_part * cycle_mask, CIL, CXL)
            for left_part, right_part in factor_pairs
        ]
    )


def local(traces, filter_taps, slot_block, slot_cells, pair_count):
    devices = lax.axis_size("il") * lax.axis_size("xl")
    samples = traces.shape[1]
    capacity = slot_block.shape[2]
    row_block = slot_cells.shape[3]
    surveys, taps = filter_taps.shape
    cell_count = CIL * CXL
    both = ("il", "xl")
    swap = functools.partial(
        lax.all_to_all, axis_name=both, split_axis=0, concat_axis=0, tiled=True
    )
    padded = jnp.pad(filter_taps, ((0, 0), (0, samples - taps)))
    rev = jnp.roll(padded[:, ::-1], 1, axis=1)
    blocks = slot_block[0].reshape(-1)
    slot_live = jnp.arange(capacity, dtype=jnp.int32)[None, :] < pair_count[0][:, None]
    out_cells = jnp.where(slot_live[:, :, None], slot_cells[0], -1)
    in_cells = swap(out_cells)
    out0, out1, filt, mats = prep(traces, rev, blocks, surveys, samples, devices)
    in0 = swap(out0)
    in1 = swap(out1)
    cells0 = in_cells[:, 0]
    cells1 = in_cells[:, 1]
    first = bin_first(cells0, in0, cell_count)
    half, image = bin_last(cells1, in1, first, cell_count)
    ans0 = read(cells0, half, samples)
    back0 = swap(ans0)
    ans1 = read(cells1, half, samples)
    back1 = swap(ans1)
    structure_tensor = tensor(image.reshape(CIL, CXL, samples))
    adjoint_traces = adjoint(
        blocks, out_cells.reshape(-1, row_block), back0, back1, filt, mats
    )
    return (structure_tensor, adjoint_traces)


def solution(mesh):
    return jax.shard_map(
        local,
        mesh=mesh,
        in_specs=(
            P(("il", "xl"), None),
            P(),
            P(("il", "xl"), None, None),
            P(("il", "xl"), None, None, None),
            P(("il", "xl"), None),
        ),
        out_specs=(P(None, "il", "xl", None), P(("il", "xl"), None)),
        check_vma=False,
    )
```

```python
import functools

import jax
import jax.numpy as jnp
from jax import lax
from jax.experimental import pallas as pl
from jax.experimental.pallas import tpu as pltpu
from jax.sharding import PartitionSpec as P

CIL = 32
CXL = 48
LOW = 256
GROUP = 8
BF = jnp.bfloat16
F32 = jnp.float32


def prep_kernel(blocks, traces, rev, cells, out, filt, mats):
    surveys = mats.shape[0]
    samples = mats.shape[1]
    rows = traces.shape[0] // surveys
    per = rows // samples
    tiles, slots = cells.shape[:2]
    part = samples // 2
    step = pl.program_id(0)

    @pl.when(step == 0)
    def _():
        t_id = lax.broadcasted_iota(jnp.int32, (samples, samples), 0)
        u_id = lax.broadcasted_iota(jnp.int32, (samples, samples), 1)
        for s in range(surveys):
            base = jnp.broadcast_to(rev[s : s + 1, :], (samples, samples))
            skew = pltpu.roll(base, 0, 1, stride=1, stride_axis=0)
            mat = jnp.where(u_id <= t_id, skew, 0.0).astype(BF)
            mats[s] = mat
            res = lax.dot_general(
                mat,
                traces[s * rows : (s + 1) * rows, :],
                (((1,), (1,)), ((), ())),
                preferred_element_type=F32,
            ).astype(BF)
            for b in range(per):
                filt[s * per + b] = res[:, b * samples : (b + 1) * samples]

    for k in range(tiles):
        for c in range(slots):
            block = blocks[(step * tiles + k) * slots + c]
            out[k, c * part : (c + 1) * part, :] = filt[block, :part, :]
        here = cells[k]
        tags = [here & (LOW - 1), here >> 8, jnp.zeros((8 - 2 * slots, samples), jnp.int32)]
        out[k, slots * part :, :] = jnp.concatenate(tags, axis=0).astype(F32).astype(BF)


def prep(traces, rev, blocks, cells, surveys):
    tiles = 8
    devices, slots, samples = cells.shape
    nblk = traces.shape[0] // samples
    part = samples // 2
    full = lambda *shape: pl.BlockSpec(shape, lambda i, *_: (0,) * len(shape))
    return pl.pallas_call(
        prep_kernel,
        grid_spec=pltpu.PrefetchScalarGridSpec(
            num_scalar_prefetch=1,
            grid=(devices // tiles,),
            in_specs=[
                full(*traces.shape),
                full(*rev.shape),
                pl.BlockSpec((tiles, slots, samples), lambda i, *_: (i, 0, 0)),
            ],
            out_specs=[
                pl.BlockSpec((tiles, slots * part + 8, samples), lambda i, *_: (i, 0, 0)),
                full(nblk, samples, samples),
                full(surveys, samples, samples),
            ],
        ),
        out_shape=[
            jax.ShapeDtypeStruct((devices, slots * part + 8, samples), BF),
            jax.ShapeDtypeStruct((nblk, samples, samples), BF),
            jax.ShapeDtypeStruct((surveys, samples, samples), BF),
        ],
        name="prep",
    )(blocks, traces, rev, cells)


def late_kernel(blocks, filt, out):
    tiles, slots, part = out.shape[:3]
    step = pl.program_id(0)
    for k in range(tiles):
        for c in range(slots):
            out[k, c] = filt[blocks[(step * tiles + k) * slots + c], part:, :]


def late(blocks, filt, devices, slots):
    tiles = 8
    nblk, samples, lanes = filt.shape
    part = samples // 2
    return pl.pallas_call(
        late_kernel,
        grid_spec=pltpu.PrefetchScalarGridSpec(
            num_scalar_prefetch=1,
            grid=(devices // tiles,),
            in_specs=[pl.BlockSpec(filt.shape, lambda i, *_: (0, 0, 0))],
            out_specs=pl.BlockSpec((tiles, slots, part, lanes), lambda i, *_: (i, 0, 0, 0)),
        ),
        out_shape=jax.ShapeDtypeStruct((devices, slots, part, lanes), BF),
        cost_estimate=pl.CostEstimate(
            flops=0, bytes_accessed=filt.size * 2 + devices * slots * part * lanes * 2,
            transcendentals=0,
        ),
        name="late",
    )(blocks, filt)


def low_hot(cells, lanes):
    ids = lax.broadcasted_iota(jnp.int32, (LOW, lanes), 0)
    return (ids == (cells & (LOW - 1))).astype(F32).astype(BF)


def fill(cells, pick, samples, left, hot):
    group, lanes = cells.shape
    highs = (left.shape[0] - 16) // samples
    ids = lax.broadcasted_iota(jnp.int32, (16, lanes), 0)
    for g in range(group):
        at = slice(g * lanes, (g + 1) * lanes)
        here = cells[g : g + 1, :]
        high = here >> 8
        hot[:, at] = low_hot(here, lanes)
        block = pick(g)
        masks = (ids == high).astype(F32).astype(BF)
        left[highs * samples :, at] = masks
        for h in range(highs):
            left[h * samples : (h + 1) * samples, at] = block * jnp.broadcast_to(
                (high == h).astype(F32).astype(BF), block.shape
            )


def accumulate(cells, pick, part, acc, left, hot):
    @pl.when(pl.program_id(0) == 0)
    def _():
        acc[...] = jnp.zeros_like(acc)

    fill(cells, pick, part, left, hot)
    acc[...] += lax.dot_general(
        left[...], hot[...], (((1,), (1,)), ((), ())), preferred_element_type=F32
    )


def divided(acc, h, part, highs):
    fold = acc[highs * part + h : highs * part + h + 1, :]
    return acc[h * part : (h + 1) * part, :] / jnp.maximum(fold, 1.0)


def bin_early_kernel(cells, data, half, value, acc, left, hot):
    slots = cells.shape[0] // data.shape[0]
    part = data.shape[1] // slots // 16 * 16

    def pick(g):
        return data[g // slots, g % slots * part : (g % slots + 1) * part, :]

    accumulate(cells, pick, part, acc, left, hot)

    @pl.when(pl.program_id(0) == pl.num_programs(0) - 1)
    def _():
        highs = half.shape[0] // part
        for h in range(highs):
            at = slice(h * part, (h + 1) * part)
            mean = divided(acc, h, part, highs)
            half[at, :] = mean.astype(BF)
            value[at, :] = mean


def bin_late_kernel(cells, data, value, half, image, acc, left, hot):
    part = data.shape[1]
    accumulate(cells, lambda g: data[g], part, acc, left, hot)

    @pl.when(pl.program_id(0) == pl.num_programs(0) - 1)
    def _():
        highs = half.shape[0] // part
        for h in range(highs):
            at = slice(h * part, (h + 1) * part)
            mean = divided(acc, h, part, highs)
            half[at, :] = mean.astype(BF)
            image[h * LOW : (h + 1) * LOW, :] = jnp.concatenate([value[at, :], mean], axis=0).T


def binned(kernel, cells, data, extra, out, name, cell_count):
    slots, lanes = cells.shape
    step = GROUP * data.shape[0] // slots
    part = data.shape[0] * data.shape[1] // slots // 16 * 16
    rows = cell_count // LOW * part
    tall = rows + 16
    whole = lambda shape: pl.BlockSpec(shape, lambda i: (0,) * len(shape))
    return pl.pallas_call(
        kernel,
        grid=(slots // GROUP,),
        in_specs=[
            pl.BlockSpec((GROUP, lanes), lambda i: (i, 0)),
            pl.BlockSpec((step, data.shape[1], lanes), lambda i: (i, 0, 0)),
        ]
        + [whole(x.shape) for x in extra],
        out_specs=[whole((rows, LOW)), whole(out)],
        out_shape=[jax.ShapeDtypeStruct((rows, LOW), BF), jax.ShapeDtypeStruct(out, F32)],
        scratch_shapes=[
            pltpu.VMEM((tall, LOW), F32),
            pltpu.VMEM((tall, GROUP * lanes), BF),
            pltpu.VMEM((LOW, GROUP * lanes), BF),
        ],
        cost_estimate=pl.CostEstimate(
            flops=2 * slots * lanes * tall * LOW, bytes_accessed=data.size * 2, transcendentals=0
        ),
        name=name,
    )(cells, data, *extra)


def read_kernel(cells, half, out, hot):
    group, part, lanes = out.shape
    highs = half.shape[0] // part
    for g in range(group):
        hot[:, g * lanes : (g + 1) * lanes] = low_hot(cells[g : g + 1, :], lanes)
    for pair in range(group // 2):
        wide = jnp.dot(
            half[...],
            hot[:, 2 * pair * lanes : 2 * (pair + 1) * lanes],
            preferred_element_type=F32,
        )
        for k in range(2):
            g = 2 * pair + k
            mine = wide[:, k * lanes : (k + 1) * lanes]
            high = jnp.broadcast_to(cells[g : g + 1, :] >> 8, (part, lanes))
            picked = jnp.zeros((part, lanes), F32)
            for h in range(highs):
                picked = jnp.where(high == h, mine[h * part : (h + 1) * part, :], picked)
            out[g] = picked.astype(BF)


def read(cells, half, part, name):
    slots, lanes = cells.shape
    return pl.pallas_call(
        read_kernel,
        grid=(slots // GROUP,),
        in_specs=[
            pl.BlockSpec((GROUP, lanes), lambda i: (i, 0)),
            pl.BlockSpec(half.shape, lambda i: (0, 0)),
        ],
        out_specs=pl.BlockSpec((GROUP, part, lanes), lambda i: (i, 0, 0)),
        out_shape=jax.ShapeDtypeStruct((slots, part, lanes), BF),
        scratch_shapes=[pltpu.VMEM((LOW, GROUP * lanes), BF)],
        cost_estimate=pl.CostEstimate(
            flops=2 * slots * lanes * half.size,
            bytes_accessed=slots * lanes * part * 2,
            transcendentals=0,
        ),
        name=name,
    )(cells, half)


def subtract(first, blocks, block_rows, cells, back, filt, acc):
    nblk, part = acc.shape[:2]
    tiles, slots = back.shape[:2]
    step = pl.program_id(0)

    @pl.when(step == 0)
    def _():
        live = (cells[...] >= 0).astype(F32).astype(BF)
        ids = lax.broadcasted_iota(jnp.int32, (64, cells.shape[0]), 0)
        pick = (ids == block_rows[...]).astype(F32).astype(BF)
        count = jnp.dot(pick, live, preferred_element_type=F32)
        for b in range(nblk):
            acc[b] = filt[b, first : first + part, :].astype(F32) * count[b : b + 1, :]

    for k in range(tiles):
        for c in range(slots):
            b = blocks[(step * tiles + k) * slots + c]
            acc[b] = acc[b] - back[k, c].astype(F32)


def misfit_kernel(blocks, block_rows, cells, back, filt, out, acc):
    subtract(0, blocks, block_rows, cells, back, filt, acc)

    @pl.when(pl.program_id(0) == pl.num_programs(0) - 1)
    def _():
        out[...] = acc[...].astype(BF)


def adjoint_kernel(blocks, block_rows, cells, back, filt, early, mats, out, acc):
    nblk, part, lanes = acc.shape
    subtract(part, blocks, block_rows, cells, back, filt, acc)
    per = nblk // mats.shape[0]

    @pl.when(pl.program_id(0) == pl.num_programs(0) - 1)
    def _():
        for b in range(nblk):
            out[b * lanes : (b + 1) * lanes, :] = lax.dot_general(
                jnp.concatenate([early[b], acc[b].astype(BF)], axis=0),
                mats[b // per],
                (((0,), (0,)), ((), ())),
                preferred_element_type=F32,
            )


def owner_call(kernel, blocks, cells, back, rest, out_shape, name):
    tiles = 8
    devices, slots, part, lanes = back.shape
    nblk = rest[0].shape[0]
    full = lambda *shape: pl.BlockSpec(shape, lambda i, *_: (0,) * len(shape))
    return pl.pallas_call(
        kernel,
        grid_spec=pltpu.PrefetchScalarGridSpec(
            num_scalar_prefetch=1,
            grid=(devices // tiles,),
            in_specs=[
                full(1, blocks.shape[0]),
                full(*cells.shape),
                pl.BlockSpec((tiles, slots, part, lanes), lambda i, *_: (i, 0, 0, 0)),
            ]
            + [full(*x.shape) for x in rest],
            out_specs=full(*out_shape.shape),
            scratch_shapes=[pltpu.VMEM((nblk, part, lanes), F32)],
        ),
        out_shape=out_shape,
        cost_estimate=pl.CostEstimate(
            flops=0, bytes_accessed=back.size * 2 + rest[0].size * 4, transcendentals=0
        ),
        name=name,
    )(blocks, blocks[None, :], cells, back, *rest)


def edges(block, axis, dim, width):
    count = lax.axis_size(axis)
    forward = [(i, i + 1) for i in range(count - 1)]
    backward = [(target, source) for source, target in forward]
    low = lax.ppermute(
        lax.slice_in_dim(block, block.shape[dim] - width, None, axis=dim), axis, forward
    )
    high = lax.ppermute(lax.slice_in_dim(block, 0, width, axis=dim), axis, backward)
    return low, high


def cycle_box(values, rows_out, cols_out):
    box_total = jnp.zeros((rows_out, cols_out, values.shape[2]), F32)
    for row_shift in range(3):
        for col_shift in range(3):
            box_total = (
                box_total
                + values[row_shift : row_shift + rows_out, col_shift : col_shift + cols_out]
            )
    return box_total / 9.0


def tensor(padded):
    count_il = lax.axis_size("il")
    count_xl = lax.axis_size("xl")
    padded_time = jnp.pad(padded, ((0, 0), (0, 0), (1, 1)))
    grad_il = (padded[2:, 1:-1] - padded[:-2, 1:-1]) * 0.5
    grad_xl = (padded[1:-1, 2:] - padded[1:-1, :-2]) * 0.5
    grad_time = (padded_time[1:-1, 1:-1, 2:] - padded_time[1:-1, 1:-1, :-2]) * 0.5
    rows_il = lax.axis_index("il") * CIL + jnp.arange(CIL + 2, dtype=jnp.int32) - 1
    rows_xl = lax.axis_index("xl") * CXL + jnp.arange(CXL + 2, dtype=jnp.int32) - 1
    inside_il = ((rows_il >= 0) & (rows_il < CIL * count_il)).astype(F32)
    inside_xl = ((rows_xl >= 0) & (rows_xl < CXL * count_xl)).astype(F32)
    cycle_mask = inside_il[:, None, None] * inside_xl[None, :, None]
    factor_pairs = (
        (grad_il, grad_il),
        (grad_xl, grad_xl),
        (grad_time, grad_time),
        (grad_il, grad_xl),
        (grad_il, grad_time),
        (grad_xl, grad_time),
    )
    return jnp.stack(
        [
            cycle_box(left_part * right_part * cycle_mask, CIL, CXL)
            for left_part, right_part in factor_pairs
        ]
    )


def local(traces, filter_taps, slot_block, slot_cells, pair_count):
    devices = lax.axis_size("il") * lax.axis_size("xl")
    rows, samples = traces.shape
    slots = slot_block.shape[2]
    lanes = slot_cells.shape[3]
    surveys, taps = filter_taps.shape
    cell_count = CIL * CXL
    part = samples // 2
    flat = (devices * slots, part, lanes)
    boxed = (devices, slots, part, lanes)
    high_rows = cell_count // LOW * part
    swap = functools.partial(
        lax.all_to_all, axis_name=("il", "xl"), split_axis=0, concat_axis=0, tiled=True
    )
    wide = jnp.pad(filter_taps, ((0, 0), (0, samples - taps)))
    rev = jnp.roll(wide[:, ::-1], 1, axis=1)
    blocks = slot_block[0].reshape(-1)
    slot_live = jnp.arange(slots, dtype=jnp.int32)[None, :] < pair_count[0][:, None]
    out_cells = jnp.where(slot_live[:, :, None], slot_cells[0], -1)
    out_early, filt, mats = prep(traces, rev, blocks, out_cells, surveys)
    in_early = swap(out_early)
    out_late = late(blocks, filt, devices, slots)
    in_late = swap(out_late)
    tags = in_early[:, slots * part :, :].astype(jnp.int32)
    cells = (tags[:, slots : 2 * slots] * LOW + tags[:, :slots]).reshape(-1, lanes)
    half_early, value = binned(
        bin_early_kernel, cells, in_early, (), (high_rows, LOW), "bin_early", cell_count
    )
    answer_early = read(cells, half_early, part, "read_early")
    back_early = swap(answer_early.reshape(boxed))
    half_late, image = binned(
        bin_late_kernel,
        cells,
        in_late.reshape(flat),
        (value,),
        (cell_count, samples),
        "bin_late",
        cell_count,
    )
    answer_late = read(cells, half_late, part, "read_late")
    tile = image.reshape(CIL, CXL, samples)
    low, high = edges(tile, "il", 0, 2)
    answer_late, low, high = lax.optimization_barrier((answer_late, low, high))
    tall = jnp.concatenate([low, tile, high], axis=0)
    low, high = edges(tall, "xl", 1, 2)
    padded = jnp.concatenate([low, tall, high], axis=1)
    answer_late, padded = lax.optimization_barrier((answer_late, padded))
    back_late = swap(answer_late.reshape(boxed))
    structure_tensor = tensor(padded)
    mine = out_cells.reshape(-1, lanes)
    early = owner_call(
        misfit_kernel,
        blocks,
        mine,
        back_early,
        (filt,),
        jax.ShapeDtypeStruct((filt.shape[0], part, lanes), BF),
        "misfit",
    )
    adjoint_traces = owner_call(
        adjoint_kernel,
        blocks,
        mine,
        back_late,
        (filt, early, mats),
        jax.ShapeDtypeStruct((rows, samples), F32),
        "adjoint",
    )
    return (structure_tensor, adjoint_traces)


def solution(mesh):
    return jax.shard_map(
        local,
        mesh=mesh,
        in_specs=(
            P(("il", "xl"), None),
            P(),
            P(("il", "xl"), None, None),
            P(("il", "xl"), None, None, None),
            P(("il", "xl"), None),
        ),
        out_specs=(P(None, "il", "xl", None), P(("il", "xl"), None)),
        check_vma=False,
    )
```

```python
import functools

import jax
import jax.numpy as jnp
from jax import lax
from jax.experimental import pallas as pl
from jax.experimental.pallas import tpu as pltpu
from jax.sharding import PartitionSpec as P

CIL = 32
CXL = 48
LOW = 256
GROUP = 32
BF = jnp.bfloat16
F32 = jnp.float32


def prep_kernel(blocks, counts, traces, taps, cells, out, filt, mats, wide):
    surveys = mats.shape[0]
    samples = mats.shape[1]
    rows = traces.shape[0] // surveys
    per = rows // samples
    tiles, slots = cells.shape[:2]
    part = samples // 2
    step = pl.program_id(0)

    @pl.when(step == 0)
    def _():
        u_id = lax.broadcasted_iota(jnp.int32, (samples, samples), 0)
        t_id = lax.broadcasted_iota(jnp.int32, (samples, samples), 1)
        wide[...] = jnp.zeros_like(wide)
        wide[:, : taps.shape[1]] = taps[...]
        for s in range(surveys):
            base = jnp.broadcast_to(wide[s : s + 1, :], (samples, samples))
            skew = pltpu.roll(base, 0, 1, stride=1, stride_axis=0)
            mat = jnp.where(u_id <= t_id, skew, 0.0).astype(BF)
            mats[s] = mat
            res = lax.dot_general(
                mat,
                traces[s * rows : (s + 1) * rows, :],
                (((0,), (1,)), ((), ())),
                preferred_element_type=F32,
            ).astype(BF)
            for b in range(per):
                filt[s * per + b] = res[:, b * samples : (b + 1) * samples]

    for k in range(tiles):
        for c in range(slots):
            block = blocks[c * (blocks.shape[0] // slots) + step * tiles + k]
            out[k, c * part : (c + 1) * part, :] = filt[block, :part, :]
        live = lax.broadcasted_iota(jnp.int32, (slots, samples), 0) < counts[step * tiles + k]
        here = jnp.where(live, cells[k], -1)
        tags = [here & (LOW - 1), here >> 8, jnp.zeros((8 - 2 * slots, samples), jnp.int32)]
        out[k, slots * part :, :] = jnp.concatenate(tags, axis=0).astype(F32).astype(BF)


def prep(traces, taps, blocks, counts, cells):
    tiles = 32
    surveys = taps.shape[0]
    devices, slots, samples = cells.shape
    nblk = traces.shape[0] // samples
    part = samples // 2
    full = lambda *shape: pl.BlockSpec(shape, lambda i, *_: (0,) * len(shape))
    return pl.pallas_call(
        prep_kernel,
        grid_spec=pltpu.PrefetchScalarGridSpec(
            num_scalar_prefetch=2,
            grid=(devices // tiles,),
            in_specs=[
                full(*traces.shape),
                full(*taps.shape),
                pl.BlockSpec((tiles, slots, samples), lambda i, *_: (i, 0, 0)),
            ],
            out_specs=[
                pl.BlockSpec((tiles, slots * part + 8, samples), lambda i, *_: (i, 0, 0)),
                full(nblk, samples, samples),
                full(surveys, samples, samples),
            ],
            scratch_shapes=[pltpu.VMEM((surveys, samples), F32)],
        ),
        out_shape=[
            jax.ShapeDtypeStruct((devices, slots * part + 8, samples), BF),
            jax.ShapeDtypeStruct((nblk, samples, samples), BF),
            jax.ShapeDtypeStruct((surveys, samples, samples), BF),
        ],
        name="prep",
    )(blocks, counts, traces, taps, cells)


def late_kernel(blocks, filt, out):
    tiles, slots, part = out.shape[:3]
    step = pl.program_id(0)
    for k in range(tiles):
        for c in range(slots):
            out[k, c] = filt[blocks[c * (blocks.shape[0] // slots) + step * tiles + k], part:, :]


def late(blocks, filt, devices, slots):
    tiles = 32
    nblk, samples, lanes = filt.shape
    part = samples // 2
    return pl.pallas_call(
        late_kernel,
        grid_spec=pltpu.PrefetchScalarGridSpec(
            num_scalar_prefetch=1,
            grid=(devices // tiles,),
            in_specs=[pl.BlockSpec(filt.shape, lambda i, *_: (0, 0, 0))],
            out_specs=pl.BlockSpec((tiles, slots, part, lanes), lambda i, *_: (i, 0, 0, 0)),
        ),
        out_shape=jax.ShapeDtypeStruct((devices, slots, part, lanes), BF),
        cost_estimate=pl.CostEstimate(
            flops=0, bytes_accessed=filt.size * 2 + devices * slots * part * lanes * 2,
            transcendentals=0,
        ),
        name="late",
    )(blocks, filt)


def low_hot(cells, lanes):
    ids = lax.broadcasted_iota(jnp.int32, (LOW, lanes), 0).astype(F32).astype(BF)
    low = jnp.broadcast_to((cells & (LOW - 1)).astype(F32).astype(BF), (LOW, lanes))
    return jnp.where(ids == low, jnp.ones((), BF), jnp.zeros((), BF))


def fill(cells, pick, samples, left, hot):
    group, lanes = cells.shape
    highs = (left.shape[0] - 16) // samples
    ids = lax.broadcasted_iota(jnp.int32, (16, lanes), 0)
    for g in range(group):
        at = slice(g * lanes, (g + 1) * lanes)
        here = cells[g : g + 1, :]
        high = here >> 8
        hot[:, at] = low_hot(here, lanes)
        block = pick(g)
        masks = (ids == high).astype(F32).astype(BF)
        left[highs * samples :, at] = masks
        for h in range(highs):
            left[h * samples : (h + 1) * samples, at] = block * jnp.broadcast_to(
                (high == h).astype(F32).astype(BF), block.shape
            )


def accumulate(cells, pick, part, acc, left, hot):
    @pl.when(pl.program_id(0) == 0)
    def _():
        acc[...] = jnp.zeros_like(acc)

    fill(cells, pick, part, left, hot)
    acc[...] += lax.dot_general(
        left[...], hot[...], (((1,), (1,)), ((), ())), preferred_element_type=F32
    )


def divided(acc, h, part, highs):
    fold = acc[highs * part + h : highs * part + h + 1, :]
    return acc[h * part : (h + 1) * part, :] / jnp.maximum(fold, 1.0)


def bin_early_kernel(cells, data, half, value, acc, left, hot):
    slots = cells.shape[0] // data.shape[0]
    part = data.shape[1] // slots // 16 * 16

    def pick(g):
        return data[g // slots, g % slots * part : (g % slots + 1) * part, :]

    accumulate(cells, pick, part, acc, left, hot)

    @pl.when(pl.program_id(0) == pl.num_programs(0) - 1)
    def _():
        highs = half.shape[0] // part
        for h in range(highs):
            at = slice(h * part, (h + 1) * part)
            mean = divided(acc, h, part, highs)
            half[at, :] = mean.astype(BF)
            value[at, :] = mean


def bin_late_kernel(cells, data, value, half, image, acc, left, hot):
    part = data.shape[1]
    accumulate(cells, lambda g: data[g], part, acc, left, hot)

    @pl.when(pl.program_id(0) == pl.num_programs(0) - 1)
    def _():
        highs = half.shape[0] // part
        for h in range(highs):
            at = slice(h * part, (h + 1) * part)
            mean = divided(acc, h, part, highs)
            half[at, :] = mean.astype(BF)
            image[h * LOW : (h + 1) * LOW, :] = jnp.concatenate([value[at, :], mean], axis=0).T


def binned(kernel, cells, data, extra, out, name, cell_count):
    slots, lanes = cells.shape
    step = GROUP * data.shape[0] // slots
    part = data.shape[0] * data.shape[1] // slots // 16 * 16
    rows = cell_count // LOW * part
    tall = rows + 16
    whole = lambda shape: pl.BlockSpec(shape, lambda i: (0,) * len(shape))
    return pl.pallas_call(
        kernel,
        grid=(slots // GROUP,),
        in_specs=[
            pl.BlockSpec((GROUP, lanes), lambda i: (i, 0)),
            pl.BlockSpec((step, data.shape[1], lanes), lambda i: (i, 0, 0)),
        ]
        + [whole(x.shape) for x in extra],
        out_specs=[whole((rows, LOW)), whole(out)],
        out_shape=[jax.ShapeDtypeStruct((rows, LOW), BF), jax.ShapeDtypeStruct(out, F32)],
        scratch_shapes=[
            pltpu.VMEM((tall, LOW), F32),
            pltpu.VMEM((tall, GROUP * lanes), BF),
            pltpu.VMEM((LOW, GROUP * lanes), BF),
        ],
        cost_estimate=pl.CostEstimate(
            flops=2 * slots * lanes * tall * LOW, bytes_accessed=data.size * 2, transcendentals=0
        ),
        name=name,
    )(cells, data, *extra)


def read_kernel(cells, half, out, hot):
    group, part, lanes = out.shape
    highs = half.shape[0] // part
    for g in range(group):
        hot[:, g * lanes : (g + 1) * lanes] = low_hot(cells[g : g + 1, :], lanes)
    for pair in range(group // 2):
        wide = jnp.dot(
            half[...],
            hot[:, 2 * pair * lanes : 2 * (pair + 1) * lanes],
            preferred_element_type=F32,
        )
        for k in range(2):
            g = 2 * pair + k
            mine = wide[:, k * lanes : (k + 1) * lanes]
            high = jnp.broadcast_to(cells[g : g + 1, :] >> 8, (part, lanes))
            picked = jnp.zeros((part, lanes), F32)
            for h in range(highs):
                picked = jnp.where(high == h, mine[h * part : (h + 1) * part, :], picked)
            out[g] = picked.astype(BF)


def read(cells, half, part, name):
    slots, lanes = cells.shape
    return pl.pallas_call(
        read_kernel,
        grid=(slots // GROUP,),
        in_specs=[
            pl.BlockSpec((GROUP, lanes), lambda i: (i, 0)),
            pl.BlockSpec(half.shape, lambda i: (0, 0)),
        ],
        out_specs=pl.BlockSpec((GROUP, part, lanes), lambda i: (i, 0, 0)),
        out_shape=jax.ShapeDtypeStruct((slots, part, lanes), BF),
        scratch_shapes=[pltpu.VMEM((LOW, GROUP * lanes), BF)],
        cost_estimate=pl.CostEstimate(
            flops=2 * slots * lanes * half.size,
            bytes_accessed=slots * lanes * part * 2,
            transcendentals=0,
        ),
        name=name,
    )(cells, half)


def subtract(blocks, block_rows, cells, back, filt, acc):
    nblk = acc.shape[0]
    tiles, slots = back.shape[:2]
    step = pl.program_id(0)

    @pl.when(step == 0)
    def _():
        live = (cells[...] >= 0).astype(F32).astype(BF)
        ids = lax.broadcasted_iota(jnp.int32, (64, cells.shape[0]), 0)
        pick = (ids == block_rows[...]).astype(F32).astype(BF)
        count = jnp.dot(pick, live, preferred_element_type=F32)
        for b in range(nblk):
            acc[b] = filt[b].astype(F32) * count[b : b + 1, :]

    for k in range(tiles):
        for c in range(slots):
            b = blocks[c * (blocks.shape[0] // slots) + step * tiles + k]
            acc[b] = acc[b] - back[k, c].astype(F32)


def misfit_kernel(blocks, block_rows, cells, back, filt, out, acc):
    subtract(blocks, block_rows, cells, back, filt, acc)

    @pl.when(pl.program_id(0) == pl.num_programs(0) - 1)
    def _():
        out[...] = acc[...].astype(BF)


def adjoint_kernel(blocks, block_rows, cells, back, filt, early, mats, out, acc):
    nblk, part, lanes = acc.shape
    subtract(blocks, block_rows, cells, back, filt, acc)
    per = nblk // mats.shape[0]

    @pl.when(pl.program_id(0) == pl.num_programs(0) - 1)
    def _():
        for b in range(nblk):
            out[b * lanes : (b + 1) * lanes, :] = lax.dot_general(
                jnp.concatenate([early[b], acc[b].astype(BF)], axis=0),
                mats[b // per],
                (((0,), (1,)), ((), ())),
                preferred_element_type=F32,
            )


def owner_call(kernel, which, blocks, block_rows, cells, back, rest, out_shape, name):
    tiles = 16
    devices, slots, part, lanes = back.shape
    nblk = rest[0].shape[0]
    full = lambda *shape: pl.BlockSpec(shape, lambda i, *_: (0,) * len(shape))
    return pl.pallas_call(
        kernel,
        grid_spec=pltpu.PrefetchScalarGridSpec(
            num_scalar_prefetch=1,
            grid=(devices // tiles,),
            in_specs=[
                full(1, blocks.shape[0]),
                full(*cells.shape),
                pl.BlockSpec((tiles, slots, part, lanes), lambda i, *_: (i, 0, 0, 0)),
            ]
            + [pl.BlockSpec((nblk, part, lanes), lambda i, *_: (0, which, 0))]
            + [full(*x.shape) for x in rest[1:]],
            out_specs=full(*out_shape.shape),
            scratch_shapes=[pltpu.VMEM((nblk, part, lanes), F32)],
        ),
        out_shape=out_shape,
        cost_estimate=pl.CostEstimate(
            flops=0, bytes_accessed=back.size * 2 + rest[0].size * 4, transcendentals=0
        ),
        name=name,
    )(blocks, block_rows, cells, back, *rest)


def edges(block, axis, dim, width):
    count = lax.axis_size(axis)
    forward = [(i, i + 1) for i in range(count - 1)]
    backward = [(target, source) for source, target in forward]
    low = lax.ppermute(
        lax.slice_in_dim(block, block.shape[dim] - width, None, axis=dim), axis, forward
    )
    high = lax.ppermute(lax.slice_in_dim(block, 0, width, axis=dim), axis, backward)
    return low, high


def cycle_box(values, rows_out, cols_out):
    box_total = jnp.zeros((rows_out, cols_out, values.shape[2]), F32)
    for row_shift in range(3):
        for col_shift in range(3):
            box_total = (
                box_total
                + values[row_shift : row_shift + rows_out, col_shift : col_shift + cols_out]
            )
    return box_total / 9.0


def tensor(padded):
    count_il = lax.axis_size("il")
    count_xl = lax.axis_size("xl")
    padded_time = jnp.pad(padded, ((0, 0), (0, 0), (1, 1)))
    grad_il = (padded[2:, 1:-1] - padded[:-2, 1:-1]) * 0.5
    grad_xl = (padded[1:-1, 2:] - padded[1:-1, :-2]) * 0.5
    grad_time = (padded_time[1:-1, 1:-1, 2:] - padded_time[1:-1, 1:-1, :-2]) * 0.5
    rows_il = lax.axis_index("il") * CIL + jnp.arange(CIL + 2, dtype=jnp.int32) - 1
    rows_xl = lax.axis_index("xl") * CXL + jnp.arange(CXL + 2, dtype=jnp.int32) - 1
    inside_il = ((rows_il >= 0) & (rows_il < CIL * count_il)).astype(F32)
    inside_xl = ((rows_xl >= 0) & (rows_xl < CXL * count_xl)).astype(F32)
    cycle_mask = inside_il[:, None, None] * inside_xl[None, :, None]
    factor_pairs = (
        (grad_il, grad_il),
        (grad_xl, grad_xl),
        (grad_time, grad_time),
        (grad_il, grad_xl),
        (grad_il, grad_time),
        (grad_xl, grad_time),
    )
    return jnp.stack(
        [
            cycle_box(left_part * right_part * cycle_mask, CIL, CXL)
            for left_part, right_part in factor_pairs
        ]
    )


def local(traces, filter_taps, slot_block, slot_cells, pair_count):
    devices = lax.axis_size("il") * lax.axis_size("xl")
    rows, samples = traces.shape
    slots = slot_block.shape[2]
    lanes = slot_cells.shape[3]
    cell_count = CIL * CXL
    part = samples // 2
    flat = (devices * slots, part, lanes)
    boxed = (devices, slots, part, lanes)
    high_rows = cell_count // LOW * part
    swap = functools.partial(
        lax.all_to_all, axis_name=("il", "xl"), split_axis=0, concat_axis=0, tiled=True
    )
    blocks = slot_block[0].T.reshape(-1)
    block_rows = slot_block[0].reshape(1, -1)
    slot_live = jnp.arange(slots, dtype=jnp.int32)[None, :] < pair_count[0][:, None]
    out_cells = jnp.where(slot_live[:, :, None], slot_cells[0], -1)
    out_early, filt, mats = prep(
        traces, filter_taps, blocks, pair_count.reshape(-1), slot_cells[0]
    )
    in_early = swap(out_early)
    out_late = late(blocks, filt, devices, slots)
    in_late = swap(out_late)
    tags = in_early[:, slots * part :, :].astype(jnp.int32)
    cells = (tags[:, slots : 2 * slots] * LOW + tags[:, :slots]).reshape(-1, lanes)
    half_early, value = binned(
        bin_early_kernel, cells, in_early, (), (high_rows, LOW), "bin_early", cell_count
    )
    answer_early = read(cells, half_early, part, "read_early")
    back_early = swap(answer_early.reshape(boxed))
    half_late, image = binned(
        bin_late_kernel,
        cells,
        in_late.reshape(flat),
        (value,),
        (cell_count, samples),
        "bin_late",
        cell_count,
    )
    answer_late = read(cells, half_late, part, "read_late")
    tile = image.reshape(CIL, CXL, samples)
    low, high = edges(tile, "il", 0, 2)
    answer_late, low, high = lax.optimization_barrier((answer_late, low, high))
    tall = jnp.concatenate([low, tile, high], axis=0)
    low, high = edges(tall, "xl", 1, 2)
    padded = jnp.concatenate([low, tall, high], axis=1)
    answer_late, padded = lax.optimization_barrier((answer_late, padded))
    back_late = swap(answer_late.reshape(boxed))
    structure_tensor = tensor(padded)
    mine = out_cells.reshape(-1, lanes)
    early = owner_call(
        misfit_kernel,
        0,
        blocks,
        block_rows,
        mine,
        back_early,
        (filt,),
        jax.ShapeDtypeStruct((filt.shape[0], part, lanes), BF),
        "misfit",
    )
    adjoint_traces = owner_call(
        adjoint_kernel,
        1,
        blocks,
        block_rows,
        mine,
        back_late,
        (filt, early, mats),
        jax.ShapeDtypeStruct((rows, samples), F32),
        "adjoint",
    )
    return (structure_tensor, adjoint_traces)


def solution(mesh):
    return jax.shard_map(
        local,
        mesh=mesh,
        in_specs=(
            P(("il", "xl"), None),
            P(),
            P(("il", "xl"), None, None),
            P(("il", "xl"), None, None, None),
            P(("il", "xl"), None),
        ),
        out_specs=(P(None, "il", "xl", None), P(("il", "xl"), None)),
        check_vma=False,
    )
```

```python
import functools

import jax
import jax.numpy as jnp
from jax import lax
from jax.experimental import pallas as pl
from jax.experimental.pallas import tpu as pltpu
from jax.sharding import PartitionSpec as P

CIL = 32
CXL = 48
LOW = 256
GROUP = 32
BF = jnp.bfloat16
F32 = jnp.float32


def prep_kernel(
    blocks, counts, traces, taps, cells, out, filt_out, mats_out, wide, filt, mats, sems
):
    surveys = mats.shape[0]
    samples = mats.shape[1]
    rows = traces.shape[0] // surveys
    per = rows // samples
    tiles, slots = cells.shape[:2]
    part = samples // 2
    step = pl.program_id(0)
    leaving = (
        pltpu.make_async_copy(filt, filt_out, sems.at[0]),
        pltpu.make_async_copy(mats, mats_out, sems.at[1]),
    )

    @pl.when(step == 0)
    def _():
        u_id = lax.broadcasted_iota(jnp.int32, (samples, samples), 0)
        t_id = lax.broadcasted_iota(jnp.int32, (samples, samples), 1)
        wide[...] = jnp.zeros_like(wide)
        wide[:, : taps.shape[1]] = taps[...]
        for s in range(surveys):
            base = jnp.broadcast_to(wide[s : s + 1, :], (samples, samples))
            skew = pltpu.roll(base, 0, 1, stride=1, stride_axis=0)
            mat = jnp.where(u_id <= t_id, skew, 0.0).astype(BF)
            mats[s] = mat
            res = lax.dot_general(
                mat,
                traces[s * rows : (s + 1) * rows, :],
                (((0,), (1,)), ((), ())),
                preferred_element_type=F32,
            ).astype(BF)
            for b in range(per):
                filt[s * per + b] = res[:, b * samples : (b + 1) * samples]
        for copy in leaving:
            copy.start()

    for k in range(tiles):
        for c in range(slots):
            block = blocks[c * (blocks.shape[0] // slots) + step * tiles + k]
            out[k, c * part : (c + 1) * part, :] = filt[block, :part, :]
        live = lax.broadcasted_iota(jnp.int32, (slots, samples), 0) < counts[step * tiles + k]
        here = jnp.where(live, cells[k], -1)
        tags = [here & (LOW - 1), here >> 8, jnp.zeros((8 - 2 * slots, samples), jnp.int32)]
        out[k, slots * part :, :] = jnp.concatenate(tags, axis=0).astype(F32).astype(BF)

    @pl.when(step == pl.num_programs(0) - 1)
    def _():
        for copy in leaving:
            copy.wait()


def prep(traces, taps, blocks, counts, cells):
    tiles = 32
    surveys = taps.shape[0]
    devices, slots, samples = cells.shape
    nblk = traces.shape[0] // samples
    part = samples // 2
    full = lambda *shape: pl.BlockSpec(shape, lambda i, *_: (0,) * len(shape))
    return pl.pallas_call(
        prep_kernel,
        grid_spec=pltpu.PrefetchScalarGridSpec(
            num_scalar_prefetch=2,
            grid=(devices // tiles,),
            in_specs=[
                full(*traces.shape),
                full(*taps.shape),
                pl.BlockSpec((tiles, slots, samples), lambda i, *_: (i, 0, 0)),
            ],
            out_specs=[
                pl.BlockSpec((tiles, slots * part + 8, samples), lambda i, *_: (i, 0, 0)),
                pl.BlockSpec(memory_space=pl.ANY),
                pl.BlockSpec(memory_space=pl.ANY),
            ],
            scratch_shapes=[
                pltpu.VMEM((surveys, samples), F32),
                pltpu.VMEM((nblk, samples, samples), BF),
                pltpu.VMEM((surveys, samples, samples), BF),
                pltpu.SemaphoreType.DMA((2,)),
            ],
        ),
        out_shape=[
            jax.ShapeDtypeStruct((devices, slots * part + 8, samples), BF),
            jax.ShapeDtypeStruct((nblk, samples, samples), BF),
            jax.ShapeDtypeStruct((surveys, samples, samples), BF),
        ],
        name="prep",
    )(blocks, counts, traces, taps, cells)


def late_kernel(blocks, filt, out):
    tiles, slots, part = out.shape[:3]
    step = pl.program_id(0)
    for k in range(tiles):
        for c in range(slots):
            out[k, c] = filt[blocks[c * (blocks.shape[0] // slots) + step * tiles + k], part:, :]


def late(blocks, filt, devices, slots):
    tiles = 32
    nblk, samples, lanes = filt.shape
    part = samples // 2
    return pl.pallas_call(
        late_kernel,
        grid_spec=pltpu.PrefetchScalarGridSpec(
            num_scalar_prefetch=1,
            grid=(devices // tiles,),
            in_specs=[pl.BlockSpec(filt.shape, lambda i, *_: (0, 0, 0))],
            out_specs=pl.BlockSpec((tiles, slots, part, lanes), lambda i, *_: (i, 0, 0, 0)),
        ),
        out_shape=jax.ShapeDtypeStruct((devices, slots, part, lanes), BF),
        cost_estimate=pl.CostEstimate(
            flops=0, bytes_accessed=filt.size * 2 + devices * slots * part * lanes * 2,
            transcendentals=0,
        ),
        name="late",
    )(blocks, filt)


def low_hot(cells, lanes):
    ids = lax.broadcasted_iota(jnp.int32, (LOW, lanes), 0).astype(F32).astype(BF)
    low = jnp.broadcast_to((cells & (LOW - 1)).astype(F32).astype(BF), (LOW, lanes))
    return jnp.where(ids == low, jnp.ones((), BF), jnp.zeros((), BF))


def fill(cells, pick, samples, left, hot):
    group, lanes = cells.shape
    highs = (left.shape[0] - 16) // samples
    ids = lax.broadcasted_iota(jnp.int32, (16, lanes), 0)
    for g in range(group):
        at = slice(g * lanes, (g + 1) * lanes)
        here = cells[g : g + 1, :]
        high = here >> 8
        hot[:, at] = low_hot(here, lanes)
        block = pick(g)
        masks = (ids == high).astype(F32).astype(BF)
        left[highs * samples :, at] = masks
        for h in range(highs):
            left[h * samples : (h + 1) * samples, at] = block * jnp.broadcast_to(
                (high == h).astype(F32).astype(BF), block.shape
            )


def accumulate(cells, pick, part, acc, left, hot):
    @pl.when(pl.program_id(0) == 0)
    def _():
        acc[...] = jnp.zeros_like(acc)

    fill(cells, pick, part, left, hot)
    acc[...] += lax.dot_general(
        left[...], hot[...], (((1,), (1,)), ((), ())), preferred_element_type=F32
    )


def divided(acc, h, part, highs):
    fold = acc[highs * part + h : highs * part + h + 1, :]
    return acc[h * part : (h + 1) * part, :] / jnp.maximum(fold, 1.0)


def bin_early_kernel(cells, data, half, value, acc, left, hot):
    slots = cells.shape[0] // data.shape[0]
    part = data.shape[1] // slots // 16 * 16

    def pick(g):
        return data[g // slots, g % slots * part : (g % slots + 1) * part, :]

    accumulate(cells, pick, part, acc, left, hot)

    @pl.when(pl.program_id(0) == pl.num_programs(0) - 1)
    def _():
        highs = half.shape[0] // part
        for h in range(highs):
            at = slice(h * part, (h + 1) * part)
            mean = divided(acc, h, part, highs)
            half[at, :] = mean.astype(BF)
            value[at, :] = mean


def bin_late_kernel(cells, data, value, half, image, acc, left, hot):
    part = data.shape[1]
    accumulate(cells, lambda g: data[g], part, acc, left, hot)

    @pl.when(pl.program_id(0) == pl.num_programs(0) - 1)
    def _():
        highs = half.shape[0] // part
        for h in range(highs):
            at = slice(h * part, (h + 1) * part)
            mean = divided(acc, h, part, highs)
            half[at, :] = mean.astype(BF)
            image[h * LOW : (h + 1) * LOW, :] = jnp.concatenate([value[at, :], mean], axis=0).T


def binned(kernel, cells, data, extra, out, name, cell_count):
    slots, lanes = cells.shape
    step = GROUP * data.shape[0] // slots
    part = data.shape[0] * data.shape[1] // slots // 16 * 16
    rows = cell_count // LOW * part
    tall = rows + 16
    whole = lambda shape: pl.BlockSpec(shape, lambda i: (0,) * len(shape))
    return pl.pallas_call(
        kernel,
        grid=(slots // GROUP,),
        in_specs=[
            pl.BlockSpec((GROUP, lanes), lambda i: (i, 0)),
            pl.BlockSpec((step, data.shape[1], lanes), lambda i: (i, 0, 0)),
        ]
        + [whole(x.shape) for x in extra],
        out_specs=[whole((rows, LOW)), whole(out)],
        out_shape=[jax.ShapeDtypeStruct((rows, LOW), BF), jax.ShapeDtypeStruct(out, F32)],
        scratch_shapes=[
            pltpu.VMEM((tall, LOW), F32),
            pltpu.VMEM((tall, GROUP * lanes), BF),
            pltpu.VMEM((LOW, GROUP * lanes), BF),
        ],
        cost_estimate=pl.CostEstimate(
            flops=2 * slots * lanes * tall * LOW, bytes_accessed=data.size * 2, transcendentals=0
        ),
        name=name,
    )(cells, data, *extra)


def read_kernel(cells, half, out, hot):
    group, part, lanes = out.shape
    highs = half.shape[0] // part
    for g in range(group):
        hot[:, g * lanes : (g + 1) * lanes] = low_hot(cells[g : g + 1, :], lanes)
    for pair in range(group // 2):
        wide = jnp.dot(
            half[...],
            hot[:, 2 * pair * lanes : 2 * (pair + 1) * lanes],
            preferred_element_type=F32,
        )
        for k in range(2):
            g = 2 * pair + k
            mine = wide[:, k * lanes : (k + 1) * lanes]
            high = jnp.broadcast_to(cells[g : g + 1, :] >> 8, (part, lanes))
            picked = jnp.zeros((part, lanes), F32)
            for h in range(highs):
                picked = jnp.where(high == h, mine[h * part : (h + 1) * part, :], picked)
            out[g] = picked.astype(BF)


def read(cells, half, part, name):
    slots, lanes = cells.shape
    return pl.pallas_call(
        read_kernel,
        grid=(slots // GROUP,),
        in_specs=[
            pl.BlockSpec((GROUP, lanes), lambda i: (i, 0)),
            pl.BlockSpec(half.shape, lambda i: (0, 0)),
        ],
        out_specs=pl.BlockSpec((GROUP, part, lanes), lambda i: (i, 0, 0)),
        out_shape=jax.ShapeDtypeStruct((slots, part, lanes), BF),
        scratch_shapes=[pltpu.VMEM((LOW, GROUP * lanes), BF)],
        cost_estimate=pl.CostEstimate(
            flops=2 * slots * lanes * half.size,
            bytes_accessed=slots * lanes * part * 2,
            transcendentals=0,
        ),
        name=name,
    )(cells, half)


def subtract(blocks, block_rows, cells, back, filt, acc):
    nblk = acc.shape[0]
    tiles, slots = back.shape[:2]
    step = pl.program_id(0)

    @pl.when(step == 0)
    def _():
        live = (cells[...] >= 0).astype(F32).astype(BF)
        ids = lax.broadcasted_iota(jnp.int32, (64, cells.shape[0]), 0)
        pick = (ids == block_rows[...]).astype(F32).astype(BF)
        count = jnp.dot(pick, live, preferred_element_type=F32)
        for b in range(nblk):
            acc[b] = filt[b].astype(F32) * count[b : b + 1, :]

    for k in range(tiles):
        for c in range(slots):
            b = blocks[c * (blocks.shape[0] // slots) + step * tiles + k]
            acc[b] = acc[b] - back[k, c].astype(F32)


def misfit_kernel(blocks, block_rows, cells, back, filt, out, acc):
    subtract(blocks, block_rows, cells, back, filt, acc)

    @pl.when(pl.program_id(0) == pl.num_programs(0) - 1)
    def _():
        out[...] = acc[...].astype(BF)


def adjoint_kernel(blocks, block_rows, cells, back, filt, early, mats, out, acc, held, sems):
    nblk, part, lanes = acc.shape
    subtract(blocks, block_rows, cells, back, filt, acc)
    per = nblk // mats.shape[0]
    piece = nblk // sems.shape[0]

    def leaving(k):
        at = pl.ds(k * piece * lanes, piece * lanes)
        return pltpu.make_async_copy(held.at[at], out.at[at], sems.at[k])

    @pl.when(pl.program_id(0) == pl.num_programs(0) - 1)
    def _():
        for b in range(nblk):
            held[b * lanes : (b + 1) * lanes, :] = lax.dot_general(
                jnp.concatenate([early[b], acc[b].astype(BF)], axis=0),
                mats[b // per],
                (((0,), (1,)), ((), ())),
                preferred_element_type=F32,
            )
            if (b + 1) % piece == 0:
                leaving(b // piece).start()
        for k in range(nblk // piece):
            leaving(k).wait()


def owner_call(kernel, which, blocks, block_rows, cells, back, rest, out_shape, name, extra=()):
    tiles = 16
    devices, slots, part, lanes = back.shape
    nblk = rest[0].shape[0]
    full = lambda *shape: pl.BlockSpec(shape, lambda i, *_: (0,) * len(shape))
    return pl.pallas_call(
        kernel,
        grid_spec=pltpu.PrefetchScalarGridSpec(
            num_scalar_prefetch=1,
            grid=(devices // tiles,),
            in_specs=[
                full(1, blocks.shape[0]),
                full(*cells.shape),
                pl.BlockSpec((tiles, slots, part, lanes), lambda i, *_: (i, 0, 0, 0)),
            ]
            + [pl.BlockSpec((nblk, part, lanes), lambda i, *_: (0, which, 0))]
            + [full(*x.shape) for x in rest[1:]],
            out_specs=pl.BlockSpec(memory_space=pl.ANY) if extra else full(*out_shape.shape),
            scratch_shapes=[pltpu.VMEM((nblk, part, lanes), F32), *extra],
        ),
        out_shape=out_shape,
        cost_estimate=pl.CostEstimate(
            flops=0, bytes_accessed=back.size * 2 + rest[0].size * 4, transcendentals=0
        ),
        name=name,
    )(blocks, block_rows, cells, back, *rest)


def edges(block, axis, dim, width):
    count = lax.axis_size(axis)
    forward = [(i, i + 1) for i in range(count - 1)]
    backward = [(target, source) for source, target in forward]
    low = lax.ppermute(
        lax.slice_in_dim(block, block.shape[dim] - width, None, axis=dim), axis, forward
    )
    high = lax.ppermute(lax.slice_in_dim(block, 0, width, axis=dim), axis, backward)
    return low, high


def cycle_box(values, rows_out, cols_out):
    box_total = jnp.zeros((rows_out, cols_out, values.shape[2]), F32)
    for row_shift in range(3):
        for col_shift in range(3):
            box_total = (
                box_total
                + values[row_shift : row_shift + rows_out, col_shift : col_shift + cols_out]
            )
    return box_total / 9.0


def tensor(padded):
    count_il = lax.axis_size("il")
    count_xl = lax.axis_size("xl")
    padded_time = jnp.pad(padded, ((0, 0), (0, 0), (1, 1)))
    grad_il = (padded[2:, 1:-1] - padded[:-2, 1:-1]) * 0.5
    grad_xl = (padded[1:-1, 2:] - padded[1:-1, :-2]) * 0.5
    grad_time = (padded_time[1:-1, 1:-1, 2:] - padded_time[1:-1, 1:-1, :-2]) * 0.5
    rows_il = lax.axis_index("il") * CIL + jnp.arange(CIL + 2, dtype=jnp.int32) - 1
    rows_xl = lax.axis_index("xl") * CXL + jnp.arange(CXL + 2, dtype=jnp.int32) - 1
    inside_il = ((rows_il >= 0) & (rows_il < CIL * count_il)).astype(F32)
    inside_xl = ((rows_xl >= 0) & (rows_xl < CXL * count_xl)).astype(F32)
    cycle_mask = inside_il[:, None, None] * inside_xl[None, :, None]
    factor_pairs = (
        (grad_il, grad_il),
        (grad_xl, grad_xl),
        (grad_time, grad_time),
        (grad_il, grad_xl),
        (grad_il, grad_time),
        (grad_xl, grad_time),
    )
    return jnp.stack(
        [
            cycle_box(left_part * right_part * cycle_mask, CIL, CXL)
            for left_part, right_part in factor_pairs
        ]
    )


def local(traces, filter_taps, slot_block, slot_cells, pair_count):
    devices = lax.axis_size("il") * lax.axis_size("xl")
    rows, samples = traces.shape
    slots = slot_block.shape[2]
    lanes = slot_cells.shape[3]
    cell_count = CIL * CXL
    part = samples // 2
    flat = (devices * slots, part, lanes)
    boxed = (devices, slots, part, lanes)
    high_rows = cell_count // LOW * part
    swap = functools.partial(
        lax.all_to_all, axis_name=("il", "xl"), split_axis=0, concat_axis=0, tiled=True
    )
    blocks = slot_block[0].T.reshape(-1)
    block_rows = slot_block[0].reshape(1, -1)
    slot_live = jnp.arange(slots, dtype=jnp.int32)[None, :] < pair_count[0][:, None]
    out_cells = jnp.where(slot_live[:, :, None], slot_cells[0], -1)
    out_early, filt, mats = prep(
        traces, filter_taps, blocks, pair_count.reshape(-1), slot_cells[0]
    )
    in_early = swap(out_early)
    out_late = late(blocks, filt, devices, slots)
    in_late = swap(out_late)
    tags = in_early[:, slots * part :, :].astype(jnp.int32)
    cells = (tags[:, slots : 2 * slots] * LOW + tags[:, :slots]).reshape(-1, lanes)
    half_early, value = binned(
        bin_early_kernel, cells, in_early, (), (high_rows, LOW), "bin_early", cell_count
    )
    answer_early = read(cells, half_early, part, "read_early")
    back_early = swap(answer_early.reshape(boxed))
    half_late, image = binned(
        bin_late_kernel,
        cells,
        in_late.reshape(flat),
        (value,),
        (cell_count, samples),
        "bin_late",
        cell_count,
    )
    answer_late = read(cells, half_late, part, "read_late")
    tile = image.reshape(CIL, CXL, samples)
    low, high = edges(tile, "il", 0, 2)
    answer_late, low, high = lax.optimization_barrier((answer_late, low, high))
    tall = jnp.concatenate([low, tile, high], axis=0)
    low, high = edges(tall, "xl", 1, 2)
    padded = jnp.concatenate([low, tall, high], axis=1)
    answer_late, padded = lax.optimization_barrier((answer_late, padded))
    back_late = swap(answer_late.reshape(boxed))
    structure_tensor = tensor(padded)
    mine = out_cells.reshape(-1, lanes)
    early = owner_call(
        misfit_kernel,
        0,
        blocks,
        block_rows,
        mine,
        back_early,
        (filt,),
        jax.ShapeDtypeStruct((filt.shape[0], part, lanes), BF),
        "misfit",
    )
    adjoint_traces = owner_call(
        adjoint_kernel,
        1,
        blocks,
        block_rows,
        mine,
        back_late,
        (filt, early, mats),
        jax.ShapeDtypeStruct((rows, samples), F32),
        "adjoint",
        (pltpu.VMEM((rows, samples), F32), pltpu.SemaphoreType.DMA((6,))),
    )
    return (structure_tensor, adjoint_traces)


def solution(mesh):
    return jax.shard_map(
        local,
        mesh=mesh,
        in_specs=(
            P(("il", "xl"), None),
            P(),
            P(("il", "xl"), None, None),
            P(("il", "xl"), None, None, None),
            P(("il", "xl"), None),
        ),
        out_specs=(P(None, "il", "xl", None), P(("il", "xl"), None)),
        check_vma=False,
    )
```
